32 devices in a mesh: blk: 8 (over z, x), rep: 4 (over y, core).
Axes of the slice: x: 2, y: 2, z: 4, core: 2. Of those that a mesh axis runs over, the one named last changes fastest.
Arguments:
- image_emb: bfloat16 [4096, 1024], P(('blk', 'rep')), may hold values from -8 to 8
- curve_emb: bfloat16 [4096, 1024], P(('blk', 'rep')), may hold values from -8 to 8
Outputs:
- loss_value: float32 [], replicated
- image_grad: float32 [4096, 1024], P(('blk', 'rep'))
- curve_grad: float32 [4096, 1024], P(('blk', 'rep'))
The draws below stay inside these ranges and needn't reach their ends.
All inputs are finite; a program needn't handle non-finite values.
Results may differ from the reference program's by a relative error of at most 0.0015.
Values may be sent and summed in bfloat16 or wider, within the bound.
No kernel may reach another device: no remote copies, remote signals or barrier semaphores. Data moves between devices by JAX's collectives and lax.ppermute only.
A program may use at most 128 MiB of HBM per device.

```python
import math
import jax
import jax.numpy as jnp
from jax import lax

D = 1024
PAIRS = 4096


def make_pair(key):
    base_key = jax.random.fold_in(key, 11)
    key_list = jax.random.split(base_key, 5)
    position = jnp.arange(PAIRS, dtype=jnp.float32) / PAIRS
    root_width = math.sqrt(D)

    def row_scales(sub_key):
        spread = jax.random.uniform(sub_key, (PAIRS,), jnp.float32)
        return jnp.exp(jnp.log(0.3) + jnp.log(10.0) * (0.5 * position + 0.5 * spread))
    image_raw = jax.random.normal(key_list[0], (PAIRS, D), jnp.float32)
    curve_raw = jax.random.normal(key_list[1], (PAIRS, D), jnp.float32)
    image_out = row_scales(key_list[3])[:, None] * image_raw / root_width
    curve_out = row_scales(key_list[4])[:, None] * curve_raw / root_width
    image_out = jnp.clip(image_out, -8.0, 8.0)
    curve_out = jnp.clip(curve_out, -8.0, 8.0)
    return (image_out, curve_out)


def draw_image_emb(key, part):
    return make_pair(key)[0].astype(jnp.bfloat16)


def draw_curve_emb(key, part):
    return make_pair(key)[1].astype(jnp.bfloat16)


def setup_inputs(seed: int = 0) -> dict:
    key_of = jax.random.split(jax.random.key(seed), 3)
    image_emb = draw_image_emb(jax.random.fold_in(key_of[2], 71), 0)
    curve_emb = draw_curve_emb(jax.random.fold_in(key_of[2], 71), 0)
    return dict(image_emb=image_emb, curve_emb=curve_emb)


def reference(image_emb, curve_emb):
    pair_count = image_emb.shape[0]
    logit_gain = math.sqrt(D)
    block_size = min(pair_count, 1024)
    block_count = pair_count // block_size
    image_blocks = image_emb.reshape(block_count, block_size, D)

    def forward_step(carried, image_rows):
        scores = jnp.dot(image_rows, curve_emb.T, preferred_element_type=jnp.float32) * logit_gain
        highest = lax.optimization_barrier(jnp.max(scores, axis=1))
        row_part = highest + jnp.log(lax.optimization_barrier(jnp.sum(jnp.exp(scores - highest[:, None]), axis=1)))
        column_high = jnp.maximum(carried[0], lax.optimization_barrier(jnp.max(scores, axis=0)))
        column_sum = carried[1] * jnp.exp(carried[0] - column_high) + lax.optimization_barrier(jnp.sum(jnp.exp(scores - column_high[None, :]), axis=0))
        return ((column_high, column_sum), row_part)
    initial = (jnp.full((pair_count,), -1e+30, jnp.float32), jnp.zeros((pair_count,), jnp.float32))
    (column_high, column_sum), row_blocks = lax.scan(forward_step, initial, image_blocks)
    row_lse = row_blocks.reshape(pair_count)
    col_lse = column_high + jnp.log(column_sum)
    positive = lax.optimization_barrier(jnp.sum(image_emb.astype(jnp.float32) * curve_emb.astype(jnp.float32), axis=1)) * logit_gain
    loss_value = (jnp.sum(row_lse - positive) + jnp.sum(col_lse - positive)) / (2.0 * pair_count)

    def backward_step(curve_acc, packed):
        image_rows, row_part = packed
        scores = jnp.dot(image_rows, curve_emb.T, preferred_element_type=jnp.float32) * logit_gain
        weight = ((jnp.exp(scores - row_part[:, None]) + jnp.exp(scores - col_lse[None, :])) * 0.5).astype(jnp.bfloat16)
        rows_grad = jnp.dot(weight, curve_emb, preferred_element_type=jnp.float32) * logit_gain
        curve_acc = curve_acc + jnp.dot(weight.T, image_rows, preferred_element_type=jnp.float32) * logit_gain
        return (curve_acc, rows_grad)
    curve_acc, image_parts = lax.scan(backward_step, jnp.zeros((pair_count, D), jnp.float32), (image_blocks, row_lse.reshape(block_count, block_size)))
    image_grad = image_parts.reshape(pair_count, D) - logit_gain * curve_emb.astype(jnp.float32)
    curve_grad = curve_acc - logit_gain * image_emb.astype(jnp.float32)
    return (loss_value, image_grad, curve_grad)
```

```python
import functools
import math

import jax
import jax.numpy as jnp
from jax import lax
from jax.experimental import pallas as pl
from jax.experimental.pallas import tpu as pltpu
from jax.sharding import PartitionSpec as P

AXES = ("blk", "rep")
F32 = jnp.float32
BF16 = jnp.bfloat16
ANY = pl.BlockSpec(memory_space=pl.ANY)
VMEM = pl.BlockSpec(memory_space=pltpu.VMEM)
LANES = 128


def subsets(bits):
    return [sum(b for i, b in enumerate(bits) if k >> i & 1) for k in range(1 << len(bits))]


def exchange(value, count, mask_even, mask_odd=None):
    mask_odd = mask_even if mask_odd is None else mask_odd
    pairs = [(i, i ^ (mask_odd if i & 1 else mask_even)) for i in range(count)]
    return lax.ppermute(value, AXES, pairs)


def cost(flops, bytes_accessed, transcendentals=0):
    return pl.CostEstimate(
        flops=int(flops), bytes_accessed=int(bytes_accessed), transcendentals=int(transcendentals)
    )


def call(kernel, outs, scratch, estimate, args, specs):
    return pl.pallas_call(
        kernel,
        out_shape=outs,
        in_specs=specs,
        out_specs=jax.tree.map(lambda _: VMEM, outs),
        scratch_shapes=scratch,
        cost_estimate=estimate,
        compiler_params=pltpu.CompilerParams(vmem_limit_bytes=60 << 20),
    )(*args)


def fetch(sources, buffer, sem, rows):
    copies = [
        pltpu.make_async_copy(source, buffer.at[pl.ds(k * rows, rows)], sem.at[k])
        for k, source in enumerate(sources)
    ]
    for copy in copies:
        copy.start()
    return copies


def row_of(column):
    wide = jnp.broadcast_to(column, (column.shape[0], LANES))
    return jnp.transpose(wide)[0:1, :]


def scores_kernel(n_img, n_cur, rows, gain, *refs):
    images, curves = refs[:n_img], refs[n_img : n_img + n_cur]
    s_ref, row_ref, col_ref, ibuf, cbuf, isem, csem = refs[n_img + n_cur :]
    icopies = fetch(images, ibuf, isem, rows)
    ccopies = fetch(curves, cbuf, csem, rows)
    for copy in icopies:
        copy.wait()
    step = 2
    highest = None
    width = step * rows
    for j in range(0, n_cur, step):
        for copy in ccopies[j : j + step]:
            copy.wait()
        block = (
            lax.dot_general(
                ibuf[...],
                cbuf[j * rows : j * rows + width, :],
                (((1,), (1,)), ((), ())),
                preferred_element_type=F32,
            )
            * gain
        )
        s_ref[:, j * rows : j * rows + width] = block
        top = jnp.max(block, axis=0, keepdims=True)
        low = jnp.sum(jnp.exp(block - top), axis=0, keepdims=True)
        lse = top + jnp.log(low)
        for k in range(step):
            col_ref[j + k : j + k + 1, :] = lse[:, k * rows : (k + 1) * rows]
        peak = jnp.max(block, axis=1, keepdims=True)
        highest = peak if highest is None else jnp.maximum(highest, peak)
    total = None
    for j in range(0, n_cur, step):
        part = jnp.sum(
            jnp.exp(s_ref[:, j * rows : j * rows + width] - highest), axis=1, keepdims=True
        )
        total = part if total is None else total + part
    lse = row_of(highest + jnp.log(total))
    for k in range(n_img):
        row_ref[k : k + 1, :] = lse[:, k * rows : (k + 1) * rows]
    own = s_ref[0:rows, 0:rows]
    eye = lax.broadcasted_iota(jnp.int32, own.shape, 0) == lax.broadcasted_iota(
        jnp.int32, own.shape, 1
    )
    positive = jnp.sum(jnp.where(eye, own, 0.0), axis=0, keepdims=True)
    row_ref[n_cur : n_cur + 1, :] = positive
    col_ref[n_cur : n_cur + 1, :] = positive


def weight_kernel(n_img, n_cur, rows, gain, *refs):
    s_ref, row_ref, col_ref = refs[:3]
    images = refs[3 : 3 + n_img]
    w_ref, sib_ref, ibuf, isem = refs[3 + n_img :]
    copies = fetch(images, ibuf, isem, rows)
    row = jnp.concatenate([row_ref[k : k + 1, :] for k in range(n_img)], axis=1)
    row = jnp.transpose(jnp.broadcast_to(row, (LANES, n_img * rows)))
    for j in range(n_cur):
        s = s_ref[:, j * rows : (j + 1) * rows]
        w = (jnp.exp(s - row) + jnp.exp(s - col_ref[j : j + 1, :])) * 0.5
        w_ref[:, j * rows : (j + 1) * rows] = w.astype(BF16)
    for copy in copies:
        copy.wait()
    half = n_cur // 2 * rows
    part = lax.dot_general(
        w_ref[:, half:], ibuf[...], (((0,), (0,)), ((), ())), preferred_element_type=F32
    )
    sib_ref[...] = (part * gain).astype(BF16)


def image_kernel(n_img, n_cur, rows, gain, *refs):
    w_ref, curves = refs[0], refs[1 : 1 + n_cur]
    own_ref = refs[1 + n_cur]
    outs = refs[2 + n_cur : 1 + n_cur + n_img]
    cbuf, csem = refs[1 + n_cur + n_img :]
    for copy in fetch(curves, cbuf, csem, rows):
        copy.wait()
    for k in reversed(range(n_img)):
        part = (
            jnp.dot(w_ref[k * rows : (k + 1) * rows, :], cbuf[...], preferred_element_type=F32)
            * gain
        )
        if k:
            outs[k - 1][...] = part.astype(BF16)
        else:
            own_ref[...] = part - gain * cbuf[0:rows, :].astype(F32)


def curve_kernel(n_img, n_cur, rows, gain, *refs):
    w_ref, sib_ref, images = refs[0], refs[1], refs[2 : 2 + n_img]
    half = n_cur // 2
    own_ref = refs[2 + n_img]
    outs = refs[3 + n_img : 2 + n_img + half]
    ibuf, isem = refs[2 + n_img + half :]
    for copy in fetch(images, ibuf, isem, rows):
        copy.wait()
    for k in reversed(range(half)):
        part = (
            lax.dot_general(
                w_ref[:, k * rows : (k + 1) * rows],
                ibuf[...],
                (((0,), (0,)), ((), ())),
                preferred_element_type=F32,
            )
            * gain
        ) + sib_ref[k * rows : (k + 1) * rows, :].astype(F32)
        if k:
            outs[k - 1][...] = part.astype(BF16)
        else:
            own_ref[...] = part - gain * ibuf[0:rows, :].astype(F32)


def log_add(parts):
    top = functools.reduce(jnp.maximum, parts)
    return top + jnp.log(sum(jnp.exp(part - top) for part in parts))


def shards(image_emb, curve_emb):
    rows, width = image_emb.shape
    gain = math.sqrt(width)
    count = lax.axis_size("blk") * lax.axis_size("rep")
    bits = [1 << k for k in range(1, count.bit_length() - 1)]
    img_masks, cur_masks = subsets(bits[1::2]), subsets(bits[0::2])
    n_img, n_cur = len(img_masks), 2 * len(cur_masks)
    assert n_img == len(cur_masks) and count == n_img * n_cur and rows == LANES
    core = (lax.axis_index("blk") * lax.axis_size("rep") + lax.axis_index("rep")) & 1

    images = [image_emb] + [exchange(image_emb, count, m) for m in img_masks[1:]]
    curves = [curve_emb] + [exchange(curve_emb, count, m) for m in cur_masks[1:]]
    curves = curves + [exchange(c, count, 1) for c in curves]

    n_rows, n_cols = n_img * rows, n_cur * rows
    stat = jax.ShapeDtypeStruct((n_cur + 8, LANES), F32)
    scores, row_part, col_part = call(
        functools.partial(scores_kernel, n_img, n_cur, rows, gain),
        [jax.ShapeDtypeStruct((n_rows, n_cols), F32), stat, stat],
        [
            pltpu.VMEM((n_rows, width), BF16),
            pltpu.VMEM((n_cols, width), BF16),
            pltpu.SemaphoreType.DMA((n_img,)),
            pltpu.SemaphoreType.DMA((n_cur,)),
        ],
        cost(2 * n_rows * n_cols * width, 4 * n_rows * n_cols, 2 * n_rows * n_cols),
        images + curves,
        [ANY] * (n_img + n_cur),
    )

    def halves(x):
        return x[:n_img], x[n_img:n_cur]

    even = core == 0
    mine = jnp.where(even, row_part, col_part)
    theirs = exchange(jnp.where(even, col_part, row_part), count, 1)
    positive = mine[n_cur : n_cur + 1] + theirs[n_cur : n_cur + 1]
    col_own, col_sib = halves(mine)
    got_own, got_sib = halves(theirs)
    first = jnp.where(even, col_own, log_add([col_own, got_sib]))
    second = jnp.where(even, got_own, log_add([col_sib, got_own]))
    part = jnp.concatenate([first, second, jnp.broadcast_to(positive, (8, LANES))], axis=0)
    parts, positives = [part[:n_cur]], [part[n_cur:]]
    for k in range(1, n_img):
        got = exchange(part, count, img_masks[k], cur_masks[k])
        order = [half * n_img + (b ^ k) for half in range(2) for b in range(n_img)]
        parts.append(jnp.concatenate([got[b : b + 1] for b in order], axis=0))
        positives.append(got[n_cur:])
    merged = log_add(parts)
    group_positive = sum(positives)[0:1]
    other = exchange(merged, count, 1)
    row_lse = jnp.where(even, merged[:n_img], other[n_img:])
    swapped = jnp.concatenate([other[n_img:], other[:n_img]], axis=0)
    col_lse = jnp.where(even, swapped, merged)

    weight, to_sib = call(
        functools.partial(weight_kernel, n_img, n_cur, rows, gain),
        [
            jax.ShapeDtypeStruct((n_rows, n_cols), BF16),
            jax.ShapeDtypeStruct((n_cols // 2, width), BF16),
        ],
        [pltpu.VMEM((n_rows, width), BF16), pltpu.SemaphoreType.DMA((n_img,))],
        cost(n_rows * n_cols * width, 4 * n_rows * n_cols, 2 * n_rows * n_cols),
        [scores, row_lse, col_lse] + images,
        [VMEM] * 3 + [ANY] * n_img,
    )
    from_sib = exchange(to_sib, count, 1)
    own = jax.ShapeDtypeStruct((rows, width), F32)
    sent = jax.ShapeDtypeStruct((rows, width), BF16)
    image_own, *image_out = call(
        functools.partial(image_kernel, n_img, n_cur, rows, gain),
        [own] + [sent] * (n_img - 1),
        [pltpu.VMEM((n_cols, width), BF16), pltpu.SemaphoreType.DMA((n_cur,))],
        cost(2 * n_rows * n_cols * width, 4 * n_rows * n_cols),
        [weight] + curves,
        [VMEM] + [ANY] * n_cur,
    )
    image_in = [exchange(v, count, m) for v, m in zip(image_out, img_masks[1:])]
    curve_own, *curve_out = call(
        functools.partial(curve_kernel, n_img, n_cur, rows, gain),
        [own] + [sent] * (n_img - 1),
        [pltpu.VMEM((n_rows, width), BF16), pltpu.SemaphoreType.DMA((n_img,))],
        cost(n_rows * n_cols * width, 4 * n_rows * n_cols),
        [weight, from_sib] + images,
        [VMEM] * 2 + [ANY] * n_img,
    )
    curve_in = [exchange(v, count, m) for v, m in zip(curve_out, cur_masks[1:])]

    share = jnp.sum(merged, axis=0, keepdims=True) - jnp.where(even, 2.0, 0.0) * group_positive
    share = jnp.broadcast_to(share, (8, LANES))
    share = share + sum(
        exchange(share, count, cur_masks[k], img_masks[k]) for k in range(1, n_img)
    )
    share = share + exchange(share, count, 1)
    loss_value = jnp.sum(share[0]) / (2.0 * count * rows)

    image_grad = image_own + sum(v.astype(F32) for v in image_in)
    curve_grad = curve_own + sum(v.astype(F32) for v in curve_in)
    return (loss_value, image_grad, curve_grad)


def solution(mesh):
    spec = P(AXES, None)
    return jax.shard_map(
        shards, mesh=mesh, in_specs=(spec, spec), out_specs=(P(), spec, spec), check_vma=False
    )
```

```python
import functools
import math

import jax
import jax.numpy as jnp
from jax import lax
from jax.experimental import pallas as pl
from jax.experimental.pallas import tpu as pltpu
from jax.sharding import PartitionSpec as P

AXES = ("blk", "rep")
F32 = jnp.float32
BF16 = jnp.bfloat16
ANY = pl.BlockSpec(memory_space=pl.ANY)
VMEM = pl.BlockSpec(memory_space=pltpu.VMEM)
LANES = 128
VLIM = 6 << 20


def subsets(bits):
    return [sum(b for i, b in enumerate(bits) if k >> i & 1) for k in range(1 << len(bits))]


def exchange(value, count, mask_even, mask_odd=None):
    mask_odd = mask_even if mask_odd is None else mask_odd
    pairs = [(i, i ^ (mask_odd if i & 1 else mask_even)) for i in range(count)]
    return lax.ppermute(value, AXES, pairs)


def cost(flops, bytes_accessed, transcendentals=0):
    return pl.CostEstimate(
        flops=int(flops), bytes_accessed=int(bytes_accessed), transcendentals=int(transcendentals)
    )


def call(kernel, outs, scratch, estimate, args, specs):
    return pl.pallas_call(
        kernel,
        out_shape=outs,
        in_specs=specs,
        out_specs=jax.tree.map(lambda _: VMEM, outs),
        scratch_shapes=scratch,
        cost_estimate=estimate,
        compiler_params=pltpu.CompilerParams(vmem_limit_bytes=VLIM),
    )(*args)


def fetch(sources, buffer, sem, rows):
    copies = [
        pltpu.make_async_copy(source, buffer.at[pl.ds(k * rows, rows)], sem.at[k])
        for k, source in enumerate(sources)
    ]
    for copy in copies:
        copy.start()
    return copies


def is_even():
    return lax.axis_index(AXES) % 2 == 0


def row_of(column):
    wide = jnp.broadcast_to(column, (column.shape[0], LANES))
    return jnp.transpose(wide)[0:1, :]


def scores_kernel(n_img, n_cur, rows, gain, *refs):
    images, curves = refs[:n_img], refs[n_img : n_img + n_cur]
    s_ref, send_ref, keep_ref, ibuf, cbuf, row_ref, col_ref, isem, csem = refs[n_img + n_cur :]
    icopies = fetch(images, ibuf, isem, rows)
    ccopies = fetch(curves, cbuf, csem, rows)
    for copy in icopies:
        copy.wait()
    step = 2
    highest = None
    width = step * rows
    for j in range(0, n_cur, step):
        for copy in ccopies[j : j + step]:
            copy.wait()
        block = (
            lax.dot_general(
                ibuf[...],
                cbuf[j * rows : j * rows + width, :],
                (((1,), (1,)), ((), ())),
                preferred_element_type=F32,
            )
            * gain
        )
        s_ref[:, j * rows : j * rows + width] = block
        top = jnp.max(block, axis=0, keepdims=True)
        low = jnp.sum(jnp.exp(block - top), axis=0, keepdims=True)
        lse = top + jnp.log(low)
        for k in range(step):
            col_ref[j + k : j + k + 1, :] = lse[:, k * rows : (k + 1) * rows]
        peak = jnp.max(block, axis=1, keepdims=True)
        highest = peak if highest is None else jnp.maximum(highest, peak)
    total = None
    for j in range(0, n_cur, step):
        part = jnp.sum(
            jnp.exp(s_ref[:, j * rows : j * rows + width] - highest), axis=1, keepdims=True
        )
        total = part if total is None else total + part
    lse = row_of(highest + jnp.log(total))
    for k in range(n_img):
        row_ref[k : k + 1, :] = lse[:, k * rows : (k + 1) * rows]
    own = s_ref[0:rows, 0:rows]
    eye = lax.broadcasted_iota(jnp.int32, own.shape, 0) == lax.broadcasted_iota(
        jnp.int32, own.shape, 1
    )
    positive = jnp.sum(jnp.where(eye, own, 0.0), axis=0, keepdims=True)
    row_ref[n_cur : n_cur + 1, :] = positive
    col_ref[n_cur : n_cur + 1, :] = positive
    even = is_even()
    send_ref[...] = jnp.where(even, col_ref[...], row_ref[...])
    keep_ref[...] = jnp.where(even, row_ref[...], col_ref[...])


def pair_kernel(n_img, keep_ref, got_ref, out_ref):
    n_cur = 2 * n_img
    keep, got = keep_ref[...], got_ref[...]
    even = is_even()
    own, sib = keep[:n_img], keep[n_img:n_cur]
    got_own, got_sib = got[:n_img], got[n_img:n_cur]
    out_ref[:n_img, :] = jnp.where(even, own, log_add([own, got_sib]))
    out_ref[n_img:n_cur, :] = jnp.where(even, got_own, log_add([sib, got_own]))
    out_ref[n_cur:, :] = keep[n_cur:] + got[n_cur:]


def group_kernel(n_img, *refs):
    parts, merged_ref, share_ref, order_ref = refs[:n_img], refs[-3], refs[-2], refs[-1]
    n_cur = 2 * n_img
    for k in range(1, n_img):
        for b in range(n_cur):
            order_ref[k, b : b + 1, :] = parts[k][b ^ k : (b ^ k) + 1, :]
    merged = log_add([parts[0][:n_cur, :]] + [order_ref[k] for k in range(1, n_img)])
    merged_ref[...] = merged
    positive = sum(part[n_cur : n_cur + 1, :] for part in parts)
    share = jnp.sum(merged, axis=0, keepdims=True) - jnp.where(is_even(), 2.0, 0.0) * positive
    share_ref[...] = jnp.broadcast_to(share, share_ref.shape)


def add_kernel(*refs):
    ins, outs = refs[: 2 * len(refs) // 3], refs[2 * len(refs) // 3 :]
    for k, out in enumerate(outs):
        out[...] = (ins[2 * k][...] + ins[2 * k + 1][...].astype(F32)).astype(out.dtype)


def weight_kernel(n_img, n_cur, rows, gain, *refs):
    s_ref, merged_ref, other_ref, c_ref, w_ref, out_ref, row_ref, col_ref = refs
    even = is_even()
    merged, other = merged_ref[...], other_ref[...]
    row_ref[...] = jnp.where(even, merged[:n_img], other[n_img:])
    col_ref[:n_img, :] = jnp.where(even, other[n_img:], merged[:n_img])
    col_ref[n_img:, :] = jnp.where(even, other[:n_img], merged[n_img:])
    row = jnp.concatenate([row_ref[k : k + 1, :] for k in range(n_img)], axis=1)
    row = jnp.transpose(jnp.broadcast_to(row, (LANES, n_img * rows)))
    for j in range(n_cur):
        s = s_ref[:, j * rows : (j + 1) * rows]
        w = (jnp.exp(s - row) + jnp.exp(s - col_ref[j : j + 1, :])) * 0.5
        w_ref[:, j * rows : (j + 1) * rows] = w.astype(BF16)
    part = jnp.dot(w_ref[(n_img - 1) * rows :, :], c_ref[...], preferred_element_type=F32)
    out_ref[...] = (part * gain).astype(BF16)


def sibling_kernel(n_img, n_cur, rows, gain, *refs):
    w_ref, i_ref, out_ref = refs
    part = lax.dot_general(
        w_ref[:, n_cur // 2 * rows :],
        i_ref[...],
        (((0,), (0,)), ((), ())),
        preferred_element_type=F32,
    )
    out_ref[...] = (part * gain).astype(BF16)


def image_kernel(n_img, n_cur, rows, gain, *refs):
    w_ref, c_ref, outs = refs[0], refs[1], refs[2:]
    part = jnp.dot(w_ref[: (n_img - 1) * rows, :], c_ref[...], preferred_element_type=F32) * gain
    for k, out in enumerate(outs):
        block = part[k * rows : (k + 1) * rows, :]
        if k == 0:
            block = block - gain * c_ref[0:rows, :].astype(F32)
        out[...] = block.astype(out.dtype)


def curve_kernel(n_img, n_cur, rows, gain, *refs):
    w_ref, sib_ref, i_ref, outs = refs[0], refs[1], refs[2], refs[3:]
    part = lax.dot_general(
        w_ref[:, : n_cur // 2 * rows],
        i_ref[...],
        (((0,), (0,)), ((), ())),
        preferred_element_type=F32,
    )
    part = part * gain + sib_ref[...].astype(F32)
    for k, out in enumerate(outs):
        block = part[k * rows : (k + 1) * rows, :]
        if k == 0:
            block = block - gain * i_ref[0:rows, :].astype(F32)
        out[...] = block.astype(out.dtype)


def scatter_sum(parts, masks, count):
    first = None
    bit = 1
    while bit < len(masks):
        got = {}
        for k in reversed(range(bit, len(masks), 2 * bit)):
            got[k] = exchange(parts[k].astype(BF16), count, masks[bit])
            if k == bit and first is None:
                first = got[k]
        args = [v for k in got for v in (parts[k - bit], got[k])]
        kinds = [
            jax.ShapeDtypeStruct(
                got[k].shape, BF16 if (k - bit) & (2 * bit) and 2 * bit < len(masks) else F32
            )
            for k in got
        ]
        sums = call(add_kernel, kinds, [], cost(0, 0), args, [VMEM] * len(args))
        for k, value in zip(got, sums):
            parts[k - bit] = value
        bit *= 2
    return parts[0], first


def log_add(parts):
    top = functools.reduce(jnp.maximum, parts)
    return top + jnp.log(sum(jnp.exp(part - top) for part in parts))


def shards(image_emb, curve_emb):
    rows, width = image_emb.shape
    gain = math.sqrt(width)
    count = lax.axis_size("blk") * lax.axis_size("rep")
    bits = [1 << k for k in range(1, count.bit_length() - 1)]
    img_masks, cur_masks = subsets(bits[1::2]), subsets(bits[0::2])
    n_img, n_cur = len(img_masks), 2 * len(cur_masks)
    assert n_img == len(cur_masks) and count == n_img * n_cur and rows == LANES

    images = [image_emb] + [exchange(image_emb, count, m) for m in img_masks[1:]]
    curves = [curve_emb] + [exchange(curve_emb, count, m) for m in cur_masks[1:]]
    curves = curves + [exchange(c, count, 1) for c in curves]

    n_rows, n_cols = n_img * rows, n_cur * rows
    stat = jax.ShapeDtypeStruct((n_cur + 8, LANES), F32)
    img_all = jax.ShapeDtypeStruct((n_rows, width), BF16)
    cur_all = jax.ShapeDtypeStruct((n_cols, width), BF16)
    flops = 2 * n_rows * n_cols * width
    scores, send, keep, image_all, curve_all = call(
        functools.partial(scores_kernel, n_img, n_cur, rows, gain),
        [jax.ShapeDtypeStruct((n_rows, n_cols), F32), stat, stat, img_all, cur_all],
        [pltpu.VMEM(stat.shape, F32)] * 2
        + [pltpu.SemaphoreType.DMA((n_img,)), pltpu.SemaphoreType.DMA((n_cur,))],
        cost(flops, 8 * n_rows * n_cols, 2 * n_rows * n_cols),
        images + curves,
        [ANY] * (n_img + n_cur),
    )

    theirs = exchange(send, count, 1)
    part = call(
        functools.partial(pair_kernel, n_img), stat, [], cost(0, 0), [keep, theirs], [VMEM] * 2
    )
    parts = [part] + [exchange(part, count, img_masks[k], cur_masks[k]) for k in range(1, n_img)]
    lse = jax.ShapeDtypeStruct((n_cur, LANES), F32)
    merged, share = call(
        functools.partial(group_kernel, n_img),
        [lse, jax.ShapeDtypeStruct((8, LANES), F32)],
        [pltpu.VMEM((n_img, n_cur, LANES), F32)],
        cost(0, 0),
        parts,
        [VMEM] * n_img,
    )
    other = exchange(merged, count, 1)

    own = jax.ShapeDtypeStruct((rows, width), F32)
    sent = jax.ShapeDtypeStruct((rows, width), BF16)
    kinds = [sent if k & 1 else own for k in range(n_img)]
    weight, image_last = call(
        functools.partial(weight_kernel, n_img, n_cur, rows, gain),
        [jax.ShapeDtypeStruct((n_rows, n_cols), BF16), kinds[-1]],
        [pltpu.VMEM((n_img, LANES), F32), pltpu.VMEM((n_cur, LANES), F32)],
        cost(flops // n_img, 6 * n_rows * n_cols, 2 * n_rows * n_cols),
        [scores, merged, other, curve_all],
        [VMEM] * 4,
    )
    to_sib = call(
        functools.partial(sibling_kernel, n_img, n_cur, rows, gain),
        jax.ShapeDtypeStruct((n_cols // 2, width), BF16),
        [],
        cost(flops // 2, 2 * n_rows * n_cols),
        [weight, image_all],
        [VMEM] * 2,
    )
    from_sib = exchange(to_sib, count, 1)
    image_parts = call(
        functools.partial(image_kernel, n_img, n_cur, rows, gain),
        kinds[:-1],
        [],
        cost(flops * (n_img - 1) // n_img, 4 * n_rows * n_cols),
        [weight, curve_all],
        [VMEM] * 2,
    )
    image_grad, image_got = scatter_sum([*image_parts, image_last], img_masks, count)
    curve_parts = call(
        functools.partial(curve_kernel, n_img, n_cur, rows, gain),
        kinds,
        [],
        cost(flops // 2, 4 * n_rows * n_cols),
        [weight, from_sib, image_all],
        [VMEM] * 3,
    )
    curve_grad, curve_got = scatter_sum(list(curve_parts), cur_masks, count)

    share, _ = lax.optimization_barrier((share, image_got))
    share = share + sum(exchange(share, count, cur_masks[k], img_masks[k]) for k in range(1, n_img))
    share = share + exchange(share, count, 1)
    loss_value = jnp.sum(share[0]) / (2.0 * count * rows)
    return (loss_value, image_grad, curve_grad)


def solution(mesh):
    spec = P(AXES, None)
    return jax.shard_map(
        shards, mesh=mesh, in_specs=(spec, spec), out_specs=(P(), spec, spec), check_vma=False
    )
```
